32 devices in a mesh: layers: 2 (over x), col: 16 (over z, y, core).
Axes of the slice: x: 2, y: 2, z: 4, core: 2. Of those that a mesh axis runs over, the one named last changes fastest.
Arguments:
- dense_weight: float32 [64, 16384], P('layers', 'col'), parts along dimension 0, may hold values from -6 to 6
- start_weight: float32 [64, 16384], P('layers', 'col'), parts along dimension 0, may hold values from -6 to 6
- keep_mask: int32 [64, 16384], P('layers', 'col'), parts along dimension 0, may hold values 0 or 1
- tile_plan: int32 [1056, 2], P(('layers', 'col')), parts along dimension 0, may hold values from 0 to 31, as said below
- hess_tiles: float32 [1056, 512, 512], P(('layers', 'col')), parts along dimension 0, as said below
Outputs:
- weights_out: float32 [64, 16384], P('layers', 'col'), parts along dimension 0
- velocity_out: float32 [64, 16384], P('layers', 'col'), parts along dimension 0
The draws below stay inside these ranges and needn't reach their ends.
There are 2 independent parts, one for each index of `layers`. The reference program is written for one: setup_inputs(seed, part) draws one part's arguments, and reference() takes and returns one part's arrays. A program takes and returns all parts, laid end to end along the dimension named above; each array names one. Nothing has to cross between parts.
Inputs may be any that keep to these rules, and one draw needn't show every extreme that they name: `tile_plan`: each live slot names a tile (a, b) with a >= b, and each of the 32 (33) / 2 lower-triangle tiles is named by exactly one slot; the other slots name (0, 0). `hess_tiles`: the tiles of a symmetric positive definite matrix at the places that tile_plan names; slots that name no tile hold zeros.
All inputs are finite; a program needn't handle non-finite values. No bound on the sum of `keep_mask` on one device may be relied on, other than what follows from the above.
Results may differ from the reference program's by a relative error of at most 0.0001.
Values sent between devices are 32-bit elements; how exact they have to be, the bound alone decides.
A program may use at most 64 MiB of HBM per device.

```python
import math
import jax
import jax.numpy as jnp
from jax import lax

K = 16384
TB = 512
R = 32
ITERS = 2
NB = 32
PLAN_ROWS = 528


def plan_parts(key):
    order = jax.random.permutation(jax.random.fold_in(key, 11), PLAN_ROWS).astype(jnp.int32)
    count = NB * (NB + 1) // 2
    live = order < count
    index = jnp.where(live, order, 0)
    blocks = jnp.arange(NB, dtype=jnp.int32)
    starts = blocks * (blocks + 1) // 2
    row_of = jnp.sum((starts[None, :] <= index[:, None]).astype(jnp.int32), axis=1) - 1
    col_of = index - row_of * (row_of + 1) // 2
    return (row_of.astype(jnp.int32), col_of.astype(jnp.int32), live)


def draw_tile_plan(key, part):
    row_of, col_of, live = plan_parts(key)
    return jnp.stack([row_of, col_of], axis=1).astype(jnp.int32)


def draw_hess_tiles(key, part):
    row_of, col_of, live = plan_parts(key)
    noise_key = jax.random.fold_in(key, 23)
    diag_key = jax.random.fold_in(key, 29)
    raw = jax.random.normal(noise_key, (PLAN_ROWS, TB, TB), jnp.float32)
    raw = raw / math.sqrt(K)
    sym = (raw + jnp.swapaxes(raw, 1, 2)) / math.sqrt(2.0)
    diag_vals = jnp.exp(jax.random.uniform(diag_key, (PLAN_ROWS, TB), jnp.float32, math.log(2.0), math.log(4.0)))
    eye = jnp.eye(TB, dtype=jnp.float32)
    diag_tile = sym + eye[None, :, :] * diag_vals[:, :, None]
    same = (row_of == col_of)[:, None, None]
    tile = jnp.where(same, diag_tile, raw)
    return tile * live[:, None, None].astype(jnp.float32)


def plant(entries, key, least, largest):
    longest = entries.shape.index(max(entries.shape))
    spots = []
    for shift in (0, 1):
        where = [jax.random.randint(jax.random.fold_in(key, axis), (), 0, length) for axis, length in enumerate(entries.shape)]
        where[longest] = (where[longest] + shift) % entries.shape[longest]
        spots.append(tuple(where))
    return entries.at[spots[0]].set(least).at[spots[1]].set(largest)


def levels(rng, shape, cuts, smallest, largest):
    gain, own = 1.0, jax.random.fold_in(rng, 6)
    for dim, parts in cuts:
        steps = jnp.exp(jax.random.uniform(jax.random.fold_in(own, dim), (parts,), jnp.float32, smallest / len(cuts), largest / len(cuts)))
        gain = gain * jnp.repeat(steps, shape[dim] // parts).reshape([-1 if axis == dim else 1 for axis in range(len(shape))])
    return gain


def gaussian(rng, dims, width, most, pieces=(), kind=jnp.bfloat16):
    array = width * jax.random.normal(rng, dims, jnp.float32)
    if pieces:
        array = array * levels(rng, dims, pieces, -0.22, 0.18)
    return jnp.clip(array, -most, most).astype(kind)


def setup_inputs(seed: int = 0, part: int = 0) -> dict:
    key_list = jax.random.split(jax.random.key(seed), 6)
    part_splits = jax.random.split(jax.random.fold_in(key_list[5], part), 6)
    dense_weight = gaussian(part_splits[0], (R, K), 1.0, 6.0, ((1, 16),), jnp.float32)
    start_weight = gaussian(part_splits[1], (R, K), 1.0, 6.0, ((1, 16),), jnp.float32)
    keep_mask = plant((jax.random.randint(part_splits[2], (R, K), 0, 2) < 1).astype(jnp.int32), jax.random.fold_in(part_splits[2], 1), 0, 1)
    tile_plan = draw_tile_plan(jax.random.fold_in(jax.random.fold_in(key_list[5], part), 71), part)
    hess_tiles = draw_hess_tiles(jax.random.fold_in(jax.random.fold_in(key_list[5], part), 71), part)
    return dict(dense_weight=dense_weight, start_weight=start_weight, keep_mask=keep_mask, tile_plan=tile_plan, hess_tiles=hess_tiles)


step_size = 0.15
momentum = 0.6


def hessian_product(error, tile_plan, hess_tiles):
    order = hess_tiles.shape[1]
    gradient = jnp.zeros(error.shape, jnp.float32)

    def one_slot(slot, acc):
        row_block = tile_plan[slot, 0]
        col_block = tile_plan[slot, 1]
        tile = hess_tiles[slot]
        left = lax.dynamic_slice_in_dim(error, row_block * order, order, 1)
        right = lax.dynamic_slice_in_dim(error, col_block * order, order, 1)
        lower = jnp.dot(left, tile, precision=lax.Precision.HIGHEST, preferred_element_type=jnp.float32)
        upper = lax.dot_general(right, tile, (((1,), (1,)), ((), ())), precision=lax.Precision.HIGHEST, preferred_element_type=jnp.float32)
        factor = (row_block != col_block).astype(jnp.float32)
        current = lax.dynamic_slice_in_dim(acc, col_block * order, order, 1)
        acc = lax.dynamic_update_slice_in_dim(acc, current + lower, col_block * order, 1)
        current = lax.dynamic_slice_in_dim(acc, row_block * order, order, 1)
        acc = lax.dynamic_update_slice_in_dim(acc, current + factor * upper, row_block * order, 1)
        return acc

    return lax.fori_loop(0, tile_plan.shape[0], one_slot, gradient)


def reference(dense_weight, start_weight, keep_mask, tile_plan, hess_tiles):
    keep = keep_mask.astype(jnp.float32)
    weights = start_weight
    velocity = jnp.zeros(start_weight.shape, jnp.float32)
    for step in range(ITERS):
        error = weights - dense_weight
        gradient = hessian_product(error, tile_plan, hess_tiles)
        velocity = momentum * velocity + gradient
        weights = keep * (weights - step_size * velocity)
    return weights, velocity
```

```python
import functools

import jax
import jax.numpy as jnp
from jax import lax
from jax.experimental import pallas as pl
from jax.experimental.pallas import tpu as pltpu
from jax.sharding import PartitionSpec as P

step_size = 0.15
momentum = 0.6
CHUNKS = 2
MESH = pl.DeviceIdType.MESH


def split(value):
    high = value.astype(jnp.bfloat16)
    return high, (value - high.astype(jnp.float32)).astype(jnp.bfloat16)


def product_kernel(plan_ref, error_ref, tiles_ref, grad_ref, pieces_ref):
    rows = error_ref.shape[1]
    group = tiles_ref.shape[0]

    @pl.when(pl.program_id(0) == 0)
    def _():
        grad_ref[...] = jnp.zeros_like(grad_ref)

        @pl.loop(0, error_ref.shape[0])
        def _(block):
            high, low = split(error_ref[block])
            pieces_ref[block, :rows, :] = high
            pieces_ref[block, rows:, :] = low

    for member in range(group):
        slot = pl.program_id(0) * group + member
        a = plan_ref[slot, 0]
        b = plan_ref[slot, 1]
        high, low = split(tiles_ref[member])

        def terms(block, tile_dim):
            dims = (((1,), (tile_dim,)), ((), ()))
            both = lax.dot_general(pieces_ref[block], high, dims, preferred_element_type=jnp.float32)
            rest = lax.dot_general(pieces_ref[block, :rows, :], low, dims, preferred_element_type=jnp.float32)
            return both[:rows] + both[rows:] + rest

        lower = terms(a, 0)
        upper = terms(b, 1)
        grad_ref[b] += lower
        grad_ref[a] += (a != b).astype(jnp.float32) * upper


def products(tile_plan, error, hess_tiles):
    slots, order, _ = hess_tiles.shape
    blocks, rows, _ = error.shape
    group = max(d for d in (1, 2, 3, 4) if slots % d == 0)
    return pl.pallas_call(
        product_kernel,
        out_shape=jax.ShapeDtypeStruct(error.shape, jnp.float32),
        grid_spec=pltpu.PrefetchScalarGridSpec(
            num_scalar_prefetch=1,
            grid=(slots // group,),
            in_specs=[
                pl.BlockSpec(memory_space=pltpu.VMEM),
                pl.BlockSpec((group, order, order), lambda i, plan: (i, 0, 0)),
            ],
            out_specs=pl.BlockSpec(memory_space=pltpu.VMEM),
            scratch_shapes=[pltpu.VMEM((blocks, 2 * rows, order), jnp.bfloat16)],
        ),
        compiler_params=pltpu.CompilerParams(dimension_semantics=("arbitrary",)),
        name="products",
    )(tile_plan, error, hess_tiles)


class Ring:
    def __init__(self, chips, sides):
        self.chips = chips
        self.sides = sides
        self.half = chips // 2
        index = lax.axis_index("col")
        self.me = index
        self.core = index % 2
        self.pos = self.place(index // 2)

    def place(self, chip):
        if self.sides == 1:
            return chip
        length = self.chips // 2
        side, depth = chip % 2, chip // 2
        return (1 - side) * depth + side * (self.chips - 1 - depth)

    def device(self, offset, core):
        pos = (self.pos + offset + self.chips) % self.chips
        if self.sides == 1:
            return pos * 2 + core
        length = self.chips // 2
        side = pos // length
        depth = (1 - side) * pos + side * (self.chips - 1 - pos)
        return (depth * 2 + side) * 2 + core

    def carries(self, distance, way, chunk):
        if 2 * distance < self.chips:
            return True
        return (chunk < CHUNKS // 2) == (way == 0)


def greet(ring):
    barrier = pltpu.get_barrier_semaphore()
    others = (ring.device(1, ring.core), ring.device(-1, ring.core), ring.device(0, 1 - ring.core))
    for other in others:
        pl.semaphore_signal(barrier, inc=1, device_id={"col": other}, device_id_type=MESH)
    pl.semaphore_wait(barrier, 3)


def remote(src, dst, send_sem, recv_sem, device):
    return pltpu.make_async_remote_copy(
        src_ref=src, dst_ref=dst, send_sem=send_sem, recv_sem=recv_sem,
        device_id={"col": device}, device_id_type=MESH,
    )


def gather(ring, whole_ref, ring_send, ring_recv, pair_send, pair_recv):
    rows = whole_ref.shape[2] // CHUNKS
    partner = ring.device(0, 1 - ring.core)
    copies = {}
    started = []

    def pair(offset, key, source, chunk):
        where = whole_ref.at[source, :, pl.ds(chunk * rows, rows), :]
        copy = remote(where, where, pair_send.at[key], pair_recv.at[key], partner)
        copy.start()
        started.append(copy)

    slot = 0
    for step in range(ring.half + 1):
        for chunk in range(CHUNKS):
            for way, sign in ((0, 1), (1, -1)):
                source = ring.device(-sign * step, ring.core)
                if step > 0:
                    if not ring.carries(step, way, chunk):
                        continue
                    copies[way, step - 1, chunk].wait_recv()
                if step < ring.half and ring.carries(step + 1, way, chunk):
                    where = whole_ref.at[source, :, pl.ds(chunk * rows, rows), :]
                    copy = remote(
                        where, where, ring_send.at[way, step, chunk], ring_recv.at[way, step, chunk],
                        ring.device(sign, ring.core),
                    )
                    copy.start()
                    copies[way, step, chunk] = copy
                if step > 0 or way == 0:
                    pair(step, slot, source, chunk)
                    slot += 1
    for copy in started:
        copy.wait()
    for copy in copies.values():
        copy.wait_send()


def scatter(ring, part_ref, mate_ref, out_ref, in_ref, ring_send, ring_recv, pair_send, pair_recv):
    rows = part_ref.shape[2] // CHUNKS
    partner = ring.device(0, 1 - ring.core)
    mates = {}
    order = [ring.half]
    for distance in range(ring.half - 1, 0, -1):
        order += [distance, -distance]
    order.append(0)
    for offset in order:
        key = offset % ring.chips
        copy = remote(
            part_ref.at[ring.device(offset, 1 - ring.core)], mate_ref.at[key],
            pair_send.at[key], pair_recv.at[key], partner,
        )
        copy.start()
        mates[key] = copy
    landed = set()
    copies = {}

    def chip_sum(offset, at):
        key = offset % ring.chips
        if key not in landed:
            mates[key].wait_recv()
            landed.add(key)
        return part_ref[ring.device(offset, ring.core), :, at, :] + mate_ref[key, :, at, :]

    for step in range(ring.half):
        distance = ring.half - step
        for chunk in range(CHUNKS):
            at = slice(chunk * rows, (chunk + 1) * rows)
            for way, sign in ((0, 1), (1, -1)):
                if not ring.carries(distance, way, chunk):
                    continue
                total = chip_sum(sign * distance, at)
                if (way, step - 1, chunk) in copies:
                    copies[way, step - 1, chunk].wait_recv()
                    total = total + in_ref[way, step - 1, :, at, :]
                out_ref[way, step, :, at, :] = total
                copy = remote(
                    out_ref.at[way, step, :, at, :], in_ref.at[way, step, :, at, :],
                    ring_send.at[way, step, chunk], ring_recv.at[way, step, chunk],
                    ring.device(sign, ring.core),
                )
                copy.start()
                copies[way, step, chunk] = copy
    sums = []
    last = ring.half - 1
    for chunk in range(CHUNKS):
        at = slice(chunk * rows, (chunk + 1) * rows)
        total = chip_sum(0, at)
        for way in (0, 1):
            if (way, last, chunk) in copies:
                copies[way, last, chunk].wait_recv()
                total = total + in_ref[way, last, :, at, :]
        sums.append((at, total))
    for copy in mates.values():
        copy.wait_send()
    for copy in copies.values():
        copy.wait_send()
    return sums


def first_kernel(chips, sides, dense_ref, start_ref, whole_ref, *sems):
    ring = Ring(chips, sides)
    subs, width = whole_ref.shape[1], whole_ref.shape[3]
    for sub in range(subs):
        at = slice(sub * width, (sub + 1) * width)
        whole_ref[ring.me, sub] = start_ref[:, at] - dense_ref[:, at]
    greet(ring)
    gather(ring, whole_ref, *sems)


def update(ring, sums, weights_ref, keep_ref, velocity_ref, weights_out, velocity_out, width, subs):
    for at, total in sums:
        for sub in range(subs):
            cols = slice(sub * width, (sub + 1) * width)
            velocity = total[sub]
            if velocity_ref is not None:
                velocity = momentum * velocity_ref[at, cols] + velocity
            velocity_out[at, cols] = velocity
            keep = keep_ref[at, cols].astype(jnp.float32)
            weights_out[at, cols] = keep * (weights_ref[at, cols] - step_size * velocity)


def middle_kernel(
    chips, sides, part_ref, dense_ref, weights_ref, keep_ref, weights_out, velocity_out, whole_ref,
    mate_ref, out_ref, in_ref, rs_send, rs_recv, rp_send, rp_recv, *sems,
):
    ring = Ring(chips, sides)
    subs, width = whole_ref.shape[1], whole_ref.shape[3]
    greet(ring)
    sums = scatter(ring, part_ref, mate_ref, out_ref, in_ref, rs_send, rs_recv, rp_send, rp_recv)
    update(ring, sums, weights_ref, keep_ref, None, weights_out, velocity_out, width, subs)
    for sub in range(subs):
        at = slice(sub * width, (sub + 1) * width)
        whole_ref[ring.me, sub] = weights_out[:, at] - dense_ref[:, at]
    gather(ring, whole_ref, *sems)


def last_kernel(
    chips, sides, part_ref, weights_ref, keep_ref, velocity_ref, weights_out, velocity_out,
    mate_ref, out_ref, in_ref, rs_send, rs_recv, rp_send, rp_recv,
):
    ring = Ring(chips, sides)
    subs, width = part_ref.shape[1], part_ref.shape[3]
    greet(ring)
    sums = scatter(ring, part_ref, mate_ref, out_ref, in_ref, rs_send, rs_recv, rp_send, rp_recv)
    update(ring, sums, weights_ref, keep_ref, velocity_ref, weights_out, velocity_out, width, subs)


def body(sides, dense_weight, start_weight, keep_mask, tile_plan, hess_tiles):
    devices = lax.axis_size("col")
    chips = devices // 2
    half = chips // 2
    rows, span = dense_weight.shape
    order = hess_tiles.shape[1]
    width = min(span, order)
    subs = span // width
    whole = (devices, subs, rows, width)
    vmem = pl.BlockSpec(memory_space=pltpu.VMEM)
    dma = pltpu.SemaphoreType.DMA
    pairs = chips * CHUNKS
    gather_sems = [dma((2, half, CHUNKS))] * 2 + [dma((pairs,))] * 2
    scatter_scratch = [
        pltpu.VMEM((chips, subs, rows, width), jnp.float32),
        pltpu.VMEM((2, half, subs, rows, width), jnp.float32),
        pltpu.VMEM((2, half, subs, rows, width), jnp.float32),
    ] + [dma((2, half, CHUNKS))] * 2 + [dma((chips,))] * 2
    local = jax.ShapeDtypeStruct((rows, span), jnp.float32)
    full = jax.ShapeDtypeStruct(whole, jnp.float32)

    def exchange(kernel, identity, inputs, outputs, scratch):
        return pl.pallas_call(
            functools.partial(kernel, chips, sides),
            out_shape=outputs,
            in_specs=[vmem] * len(inputs),
            out_specs=[vmem] * len(outputs),
            scratch_shapes=scratch,
            compiler_params=pltpu.CompilerParams(collective_id=identity, has_side_effects=True),
            name=kernel.__name__,
        )(*inputs)

    per_block = order // width

    def hessian_product(error):
        if per_block == 1:
            blocked = error.reshape(devices * subs, rows, width)
        else:
            blocked = error.reshape(-1, per_block, rows, width).transpose(0, 2, 1, 3).reshape(-1, rows, order)
        grad = products(tile_plan, blocked, hess_tiles)
        if per_block > 1:
            grad = grad.reshape(-1, rows, per_block, width).transpose(0, 2, 1, 3)
        return grad.reshape(whole)

    (error,) = exchange(first_kernel, 0, (dense_weight, start_weight), (full,), gather_sems)
    weights, velocity, error = exchange(
        middle_kernel, 1, (hessian_product(error), dense_weight, start_weight, keep_mask),
        (local, local, full), scatter_scratch + gather_sems,
    )
    weights, velocity = exchange(
        last_kernel, 2, (hessian_product(error), weights, keep_mask, velocity), (local, local), scatter_scratch,
    )
    return weights, velocity


def ring_sides(mesh):
    line = mesh.devices.reshape(-1, mesh.shape["col"])[0]
    try:
        return 2 if len({d.coords[1] for d in line}) == 2 else 1
    except AttributeError:
        return 1


def solution(mesh):
    placed = (
        P("layers", "col"),
        P("layers", "col"),
        P("layers", "col"),
        P(("layers", "col"), None),
        P(("layers", "col"), None, None),
    )
    return jax.shard_map(
        functools.partial(body, ring_sides(mesh)),
        mesh=mesh,
        in_specs=placed,
        out_specs=(P("layers", "col"), P("layers", "col")),
        check_vma=False,
    )
```

```python
import functools

import jax
import jax.numpy as jnp
from jax import lax
from jax.experimental import pallas as pl
from jax.experimental.pallas import tpu as pltpu
from jax.sharding import PartitionSpec as P

step_size = 0.15
momentum = 0.6
CHUNKS = 4
MESH = pl.DeviceIdType.MESH


def split(value):
    high = value.astype(jnp.bfloat16)
    return high, (value - high.astype(jnp.float32)).astype(jnp.bfloat16)


def product_kernel(plan_ref, error_ref, tiles_ref, grad_ref, pieces_ref):
    rows = error_ref.shape[1]
    group = tiles_ref.shape[0]

    @pl.when(pl.program_id(0) == 0)
    def _():
        grad_ref[...] = jnp.zeros_like(grad_ref)

        @pl.loop(0, error_ref.shape[0])
        def _(block):
            high, low = split(error_ref[block])
            pieces_ref[block, :rows, :] = high
            pieces_ref[block, rows:, :] = low

    for member in range(group):
        slot = pl.program_id(0) * group + member
        a = plan_ref[slot, 0]
        b = plan_ref[slot, 1]
        high, low = split(tiles_ref[member])

        def terms(block, tile_dim):
            dims = (((1,), (tile_dim,)), ((), ()))
            both = lax.dot_general(pieces_ref[block], high, dims, preferred_element_type=jnp.float32)
            rest = lax.dot_general(pieces_ref[block, :rows, :], low, dims, preferred_element_type=jnp.float32)
            return both[:rows] + both[rows:] + rest

        lower = terms(a, 0)
        upper = terms(b, 1)
        grad_ref[b] += lower
        grad_ref[a] += (a != b).astype(jnp.float32) * upper


def products(tile_plan, error, hess_tiles):
    slots, order, _ = hess_tiles.shape
    blocks, rows, _ = error.shape
    group = max(d for d in (1, 2, 3, 4) if slots % d == 0)
    return pl.pallas_call(
        product_kernel,
        out_shape=jax.ShapeDtypeStruct(error.shape, jnp.float32),
        grid_spec=pltpu.PrefetchScalarGridSpec(
            num_scalar_prefetch=1,
            grid=(slots // group,),
            in_specs=[
                pl.BlockSpec(memory_space=pltpu.VMEM),
                pl.BlockSpec((group, order, order), lambda i, plan: (i, 0, 0)),
            ],
            out_specs=pl.BlockSpec(memory_space=pltpu.VMEM),
            scratch_shapes=[pltpu.VMEM((blocks, 2 * rows, order), jnp.bfloat16)],
        ),
        compiler_params=pltpu.CompilerParams(dimension_semantics=("arbitrary",)),
        name="products",
    )(tile_plan, error, hess_tiles)


class Ring:
    def __init__(self, chips, sides):
        self.chips = chips
        self.sides = sides
        self.half = chips // 2
        index = lax.axis_index("col")
        self.me = index
        self.core = index % 2
        self.pos = self.place(index // 2)

    def place(self, chip):
        if self.sides == 1:
            return chip
        length = self.chips // 2
        side, depth = chip % 2, chip // 2
        return (1 - side) * depth + side * (self.chips - 1 - depth)

    def device(self, offset, core):
        pos = (self.pos + offset + self.chips) % self.chips
        if self.sides == 1:
            return pos * 2 + core
        length = self.chips // 2
        side = pos // length
        depth = (1 - side) * pos + side * (self.chips - 1 - pos)
        return (depth * 2 + side) * 2 + core

    def carries(self, distance, way, chunk):
        if 2 * distance < self.chips:
            return True
        return (chunk < CHUNKS // 2) == (way == 0)


def greet(ring):
    barrier = pltpu.get_barrier_semaphore()
    others = (ring.device(1, ring.core), ring.device(-1, ring.core), ring.device(0, 1 - ring.core))
    for other in others:
        pl.semaphore_signal(barrier, inc=1, device_id={"col": other}, device_id_type=MESH)
    pl.semaphore_wait(barrier, 3)


def remote(src, dst, send_sem, recv_sem, device):
    return pltpu.make_async_remote_copy(
        src_ref=src, dst_ref=dst, send_sem=send_sem, recv_sem=recv_sem,
        device_id={"col": device}, device_id_type=MESH,
    )


def gather(ring, whole_ref, ring_send, ring_recv, pair_send, pair_recv):
    rows = whole_ref.shape[2] // CHUNKS
    partner = ring.device(0, 1 - ring.core)
    copies = {}
    started = []

    def pair(offset, key, source, chunk):
        where = whole_ref.at[source, :, pl.ds(chunk * rows, rows), :]
        copy = remote(where, where, pair_send.at[key], pair_recv.at[key], partner)
        copy.start()
        started.append(copy)

    slot = 0
    for step in range(ring.half + 1):
        for chunk in range(CHUNKS):
            for way, sign in ((0, 1), (1, -1)):
                source = ring.device(-sign * step, ring.core)
                if step > 0:
                    if not ring.carries(step, way, chunk):
                        continue
                    copies[way, step - 1, chunk].wait_recv()
                if step < ring.half and ring.carries(step + 1, way, chunk):
                    where = whole_ref.at[source, :, pl.ds(chunk * rows, rows), :]
                    copy = remote(
                        where, where, ring_send.at[way, step, chunk], ring_recv.at[way, step, chunk],
                        ring.device(sign, ring.core),
                    )
                    copy.start()
                    copies[way, step, chunk] = copy
                if step > 0 or way == 0:
                    pair(step, slot, source, chunk)
                    slot += 1
    for copy in started:
        copy.wait()
    for copy in copies.values():
        copy.wait_send()


def scatter(ring, part_ref, mate_ref, out_ref, in_ref, ring_send, ring_recv, pair_send, pair_recv):
    rows = part_ref.shape[2] // CHUNKS
    partner = ring.device(0, 1 - ring.core)
    mates = {}
    order = [ring.half]
    for distance in range(ring.half - 1, 0, -1):
        order += [distance, -distance]
    order.append(0)
    for offset in order:
        key = offset % ring.chips
        copy = remote(
            part_ref.at[ring.device(offset, 1 - ring.core)], mate_ref.at[key],
            pair_send.at[key], pair_recv.at[key], partner,
        )
        copy.start()
        mates[key] = copy
    landed = set()
    copies = {}

    def chip_sum(offset, at):
        key = offset % ring.chips
        if key not in landed:
            mates[key].wait_recv()
            landed.add(key)
        return part_ref[ring.device(offset, ring.core), :, at, :] + mate_ref[key, :, at, :]

    for step in range(ring.half):
        distance = ring.half - step
        for chunk in range(CHUNKS):
            at = slice(chunk * rows, (chunk + 1) * rows)
            for way, sign in ((0, 1), (1, -1)):
                if not ring.carries(distance, way, chunk):
                    continue
                total = chip_sum(sign * distance, at)
                if (way, step - 1, chunk) in copies:
                    copies[way, step - 1, chunk].wait_recv()
                    total = total + in_ref[way, step - 1, :, at, :]
                out_ref[way, step, :, at, :] = total
                copy = remote(
                    out_ref.at[way, step, :, at, :], in_ref.at[way, step, :, at, :],
                    ring_send.at[way, step, chunk], ring_recv.at[way, step, chunk],
                    ring.device(sign, ring.core),
                )
                copy.start()
                copies[way, step, chunk] = copy
    sums = []
    last = ring.half - 1
    for chunk in range(CHUNKS):
        at = slice(chunk * rows, (chunk + 1) * rows)
        total = chip_sum(0, at)
        for way in (0, 1):
            if (way, last, chunk) in copies:
                copies[way, last, chunk].wait_recv()
                total = total + in_ref[way, last, :, at, :]
        sums.append((at, total))
    for copy in mates.values():
        copy.wait_send()
    for copy in copies.values():
        copy.wait_send()
    return sums


def first_kernel(chips, sides, dense_ref, start_ref, whole_ref, *sems):
    ring = Ring(chips, sides)
    subs, width = whole_ref.shape[1], whole_ref.shape[3]
    for sub in range(subs):
        at = slice(sub * width, (sub + 1) * width)
        whole_ref[ring.me, sub] = start_ref[:, at] - dense_ref[:, at]
    greet(ring)
    gather(ring, whole_ref, *sems)


def update(sums, weights_ref, keep_ref, weights_out, velocity_out, width, subs):
    for at, total in sums:
        for sub in range(subs):
            cols = slice(sub * width, (sub + 1) * width)
            velocity_out[at, cols] = total[sub]
            keep = keep_ref[at, cols].astype(jnp.float32)
            weights_out[at, cols] = keep * (weights_ref[at, cols] - step_size * total[sub])


def middle_kernel(
    chips, sides, part_ref, dense_ref, weights_ref, keep_ref, weights_out, velocity_out, whole_ref,
    mate_ref, out_ref, in_ref, rs_send, rs_recv, rp_send, rp_recv, *sems,
):
    ring = Ring(chips, sides)
    subs, width = whole_ref.shape[1], whole_ref.shape[3]
    greet(ring)
    sums = scatter(ring, part_ref, mate_ref, out_ref, in_ref, rs_send, rs_recv, rp_send, rp_recv)
    update(sums, weights_ref, keep_ref, weights_out, velocity_out, width, subs)
    for sub in range(subs):
        at = slice(sub * width, (sub + 1) * width)
        whole_ref[ring.me, sub] = weights_out[:, at] - dense_ref[:, at]
    gather(ring, whole_ref, *sems)


def last_kernel(
    chips, sides, part_ref, gradient_out, mate_ref, out_ref, in_ref, rs_send, rs_recv, rp_send, rp_recv,
):
    ring = Ring(chips, sides)
    subs, width = part_ref.shape[1], part_ref.shape[3]
    greet(ring)
    for at, total in scatter(ring, part_ref, mate_ref, out_ref, in_ref, rs_send, rs_recv, rp_send, rp_recv):
        for sub in range(subs):
            gradient_out[at, sub * width : (sub + 1) * width] = total[sub]


def body(sides, dense_weight, start_weight, keep_mask, tile_plan, hess_tiles):
    devices = lax.axis_size("col")
    chips = devices // 2
    half = chips // 2
    rows, span = dense_weight.shape
    order = hess_tiles.shape[1]
    width = min(span, order)
    subs = span // width
    whole = (devices, subs, rows, width)
    vmem = pl.BlockSpec(memory_space=pltpu.VMEM)
    dma = pltpu.SemaphoreType.DMA
    pairs = chips * CHUNKS
    gather_sems = [dma((2, half, CHUNKS))] * 2 + [dma((pairs,))] * 2
    scatter_scratch = [
        pltpu.VMEM((chips, subs, rows, width), jnp.float32),
        pltpu.VMEM((2, half, subs, rows, width), jnp.float32),
        pltpu.VMEM((2, half, subs, rows, width), jnp.float32),
    ] + [dma((2, half, CHUNKS))] * 2 + [dma((chips,))] * 2
    local = jax.ShapeDtypeStruct((rows, span), jnp.float32)
    full = jax.ShapeDtypeStruct(whole, jnp.float32)

    def exchange(kernel, identity, inputs, outputs, scratch):
        return pl.pallas_call(
            functools.partial(kernel, chips, sides),
            out_shape=outputs,
            in_specs=[vmem] * len(inputs),
            out_specs=[vmem] * len(outputs),
            scratch_shapes=scratch,
            compiler_params=pltpu.CompilerParams(collective_id=identity, has_side_effects=True),
            name=kernel.__name__,
        )(*inputs)

    per_block = order // width

    def hessian_product(error):
        if per_block == 1:
            blocked = error.reshape(devices * subs, rows, width)
        else:
            blocked = error.reshape(-1, per_block, rows, width).transpose(0, 2, 1, 3).reshape(-1, rows, order)
        grad = products(tile_plan, blocked, hess_tiles)
        if per_block > 1:
            grad = grad.reshape(-1, rows, per_block, width).transpose(0, 2, 1, 3)
        return grad.reshape(whole)

    (error,) = exchange(first_kernel, 0, (dense_weight, start_weight), (full,), gather_sems)
    weights, velocity, error = exchange(
        middle_kernel, 1, (hessian_product(error), dense_weight, start_weight, keep_mask),
        (local, local, full), scatter_scratch + gather_sems,
    )
    (gradient,) = exchange(last_kernel, 2, (hessian_product(error),), (local,), scatter_scratch)
    velocity = momentum * velocity + gradient
    weights = keep_mask.astype(jnp.float32) * (weights - step_size * velocity)
    return weights, velocity


def ring_sides(mesh):
    line = mesh.devices.reshape(-1, mesh.shape["col"])[0]
    try:
        return 2 if len({d.coords[1] for d in line}) == 2 else 1
    except AttributeError:
        return 1


def solution(mesh):
    placed = (
        P("layers", "col"),
        P("layers", "col"),
        P("layers", "col"),
        P(("layers", "col"), None),
        P(("layers", "col"), None, None),
    )
    return jax.shard_map(
        functools.partial(body, ring_sides(mesh)),
        mesh=mesh,
        in_specs=placed,
        out_specs=(P("layers", "col"), P("layers", "col")),
        check_vma=False,
    )
```
